32 devices in a mesh: clip: 8 (over z, x), row: 4 (over y, core).
Axes of the slice: x: 2, y: 2, z: 4, core: 2. Of those that a mesh axis runs over, the one named last changes fastest.
Arguments:
- features: bfloat16 [8, 128, 32, 256], P('clip', None, 'row'), may hold values from -6 to 6
- out_weight: bfloat16 [3, 128, 3, 3], replicated, may hold values from -0.1875 to 0.1875
- out_bias: float32 [3], replicated, may hold values from -0.5 to 0.5
- targets: bfloat16 [8, 3, 32, 256], P('clip', None, 'row'), may hold values from -1 to 1
- weight_one: bfloat16 [64, 3, 3, 3], replicated, may hold values from -1.25 to 1.25
- bias_one: float32 [64], replicated, may hold values from -0.2 to 0.2
- weight_two: bfloat16 [64, 64, 3, 3], replicated, may hold values from -0.375 to 0.375
- bias_two: float32 [64], replicated, may hold values from -0.2 to 0.2
- weight_three: bfloat16 [128, 64, 3, 3], replicated, may hold values from -0.375 to 0.375
- bias_three: float32 [128], replicated, may hold values from -0.2 to 0.2
- weight_four: bfloat16 [128, 128, 3, 3], replicated, may hold values from -0.25 to 0.25
- bias_four: float32 [128], replicated, may hold values from -0.2 to 0.2
- lin_one: float32 [64], replicated, may hold values from 0.05 to 0.5
- lin_two: float32 [128], replicated, may hold values from 0.05 to 0.5
Outputs:
- loss: float32 [], replicated
- feature_grad: bfloat16 [8, 128, 32, 256], P('clip', None, 'row')
- out_weight_grad: float32 [3, 128, 3, 3], replicated
- out_bias_grad: float32 [3], replicated
The draws below stay inside these ranges and needn't reach their ends.
All inputs are finite; a program needn't handle non-finite values.
Results may differ from the reference program's by a relative error of at most 0.02.
Values may be sent and summed in bfloat16 or wider, within the bound.
No kernel may reach another device: no remote copies, remote signals or barrier semaphores. Data moves between devices by JAX's collectives and lax.ppermute only.
A program may use at most 64 MiB of HBM per device.

```python
import math
import jax
import jax.numpy as jnp
from jax import lax

CF = 128
C1 = 64
C2 = 128
W = 256
H = 32
FRAMES = 8


def shard_levels(own_key, extent, split, least, top_value):
    def one(dim, blocks):
        steps = jax.random.uniform(jax.random.fold_in(jax.random.fold_in(own_key, 6), dim), (blocks,), jnp.float32, least / len(split), top_value / len(split))
        return jnp.repeat(jnp.exp(steps), extent[dim] // blocks).reshape((-1,) + (1,) * (len(extent) - dim - 1))

    gain = one(*split[0])
    for cut in split[1:]:
        gain = gain * one(*cut)
    return gain


def gaussian(rng, dims, scale, limit, shards=(), kind=jnp.bfloat16):
    entries = scale * jax.random.normal(rng, dims, jnp.float32)
    if shards:
        entries = entries * shard_levels(rng, dims, shards, -0.22, 0.18)
    return jnp.clip(entries, -limit, limit).astype(kind)


def setup_inputs(seed: int = 0) -> dict:
    streams_of = jax.random.split(jax.random.key(seed), 15)
    features = gaussian(streams_of[0], (FRAMES, CF, H, W), 1.0, 6.0, ((0, 8), (2, 4)))
    out_weight = gaussian(streams_of[1], (3, CF, 3, 3), (9 * CF) ** -0.5, 0.1875)
    out_bias = jnp.clip(jax.random.uniform(streams_of[2], (3,), jnp.float32, -0.5, 0.5), -0.5, 0.5)
    targets = jnp.clip(jax.random.uniform(streams_of[3], (FRAMES, 3, H, W), jnp.float32, -1.0, 1.0) * shard_levels(streams_of[3], (FRAMES, 3, H, W), ((0, 8), (2, 4)), -0.4, 0.0), -1.0, 1.0).astype(jnp.bfloat16)
    weight_one = gaussian(streams_of[4], (C1, 3, 3, 3), 27 ** -0.5, 1.25)
    bias_one = jnp.clip(jax.random.uniform(streams_of[5], (C1,), jnp.float32, -0.2, 0.2), -0.2, 0.2)
    weight_two = gaussian(streams_of[6], (C1, C1, 3, 3), (9 * C1 // 2) ** -0.5, 0.375)
    bias_two = jnp.clip(jax.random.uniform(streams_of[7], (C1,), jnp.float32, -0.2, 0.2), -0.2, 0.2)
    weight_three = gaussian(streams_of[8], (C2, C1, 3, 3), (9 * C1 // 2) ** -0.5, 0.375)
    bias_three = jnp.clip(jax.random.uniform(streams_of[9], (C2,), jnp.float32, -0.2, 0.2), -0.2, 0.2)
    weight_four = gaussian(streams_of[10], (C2, C2, 3, 3), (9 * C2 // 2) ** -0.5, 0.25)
    bias_four = jnp.clip(jax.random.uniform(streams_of[11], (C2,), jnp.float32, -0.2, 0.2), -0.2, 0.2)
    lin_one = jnp.clip(jnp.exp(jax.random.uniform(streams_of[12], (C1,), jnp.float32, math.log(0.05), math.log(0.5))), 0.05, 0.5)
    lin_two = jnp.clip(jnp.exp(jax.random.uniform(streams_of[13], (C2,), jnp.float32, math.log(0.05), math.log(0.5))), 0.05, 0.5)
    return {"features": features, "out_weight": out_weight, "out_bias": out_bias, "targets": targets, "weight_one": weight_one, "bias_one": bias_one, "weight_two": weight_two, "bias_two": bias_two, "weight_three": weight_three, "bias_three": bias_three, "weight_four": weight_four, "bias_four": bias_four, "lin_one": lin_one, "lin_two": lin_two}


shift_values = [-0.03, -0.088, -0.188]
scale_values = [0.458, 0.448, 0.45]

def shift_array():
    return jnp.array(shift_values, jnp.float32).reshape(1, 3, 1, 1)

def scale_array():
    return jnp.array(scale_values, jnp.float32).reshape(1, 3, 1, 1)

def gelu_exact(values):
    return values * 0.5 * (1.0 + jax.scipy.special.erf(values / math.sqrt(2.0)))

def gelu_slope(values):
    normal_cdf = 0.5 * (1.0 + jax.scipy.special.erf(values / math.sqrt(2.0)))
    density = jnp.exp(-0.5 * values * values) / math.sqrt(2.0 * math.pi)
    return normal_cdf + values * density

def pad_rows(inputs):
    return jnp.pad(inputs, ((0, 0), (0, 0), (1, 1), (0, 0)))

def flipped(weight):
    return jnp.flip(weight, (2, 3)).transpose(1, 0, 2, 3)

def conv_valid(padded, weight):
    frame_count, channels, row_total, col_count = padded.shape
    row_count = row_total - 2
    outputs = weight.shape[0]
    wide = jnp.pad(padded, ((0, 0), (0, 0), (0, 0), (1, 1)))
    results = []
    for frame_pos in range(frame_count):
        total = jnp.zeros((outputs, row_count * col_count), jnp.float32)
        for row_shift in range(3):
            for col_shift in range(3):
                piece = wide[frame_pos, :, row_shift:row_shift + row_count, col_shift:col_shift + col_count]
                total = total + jnp.dot(weight[:, :, row_shift, col_shift], piece.reshape(channels, row_count * col_count), preferred_element_type=jnp.float32)
        results.append(total.reshape(outputs, row_count, col_count))
    return jnp.stack(results)

def grad_from_input(grad_out, padded):
    frame_count, channels, row_total, col_count = padded.shape
    row_count = row_total - 2
    outputs = grad_out.shape[1]
    wide = jnp.pad(padded, ((0, 0), (0, 0), (0, 0), (1, 1)))
    blocks = []
    for row_shift in range(3):
        for col_shift in range(3):
            total = jnp.zeros((outputs, channels), jnp.float32)
            for frame_pos in range(frame_count):
                piece = wide[frame_pos, :, row_shift:row_shift + row_count, col_shift:col_shift + col_count].reshape(channels, row_count * col_count)
                left = grad_out[frame_pos].reshape(outputs, row_count * col_count)
                total = total + lax.dot_general(left, piece, (((1,), (1,)), ((), ())), preferred_element_type=jnp.float32)
            blocks.append(total)
    return jnp.stack(blocks).reshape(3, 3, outputs, channels).transpose(2, 3, 0, 1)

def pool_mean(values):
    frame_count, channels, row_count, col_count = values.shape
    return values.reshape(frame_count, channels, row_count // 2, 2, col_count // 2, 2).mean(axis=(3, 5))

def upsample(values):
    return jnp.repeat(jnp.repeat(values, 2, 2), 2, 3)

def vgg_forward(image, weights):
    weight_one, bias_one, weight_two, bias_two, weight_three, bias_three, weight_four, bias_four = weights
    pre_one = conv_valid(pad_rows(image), weight_one) + bias_one[None, :, None, None]
    act_one = gelu_exact(pre_one).astype(jnp.bfloat16)
    pre_two = conv_valid(pad_rows(act_one), weight_two) + bias_two[None, :, None, None]
    act_two = gelu_exact(pre_two)
    pooled = pool_mean(act_two).astype(jnp.bfloat16)
    pre_three = conv_valid(pad_rows(pooled), weight_three) + bias_three[None, :, None, None]
    act_three = gelu_exact(pre_three).astype(jnp.bfloat16)
    pre_four = conv_valid(pad_rows(act_three), weight_four) + bias_four[None, :, None, None]
    act_four = gelu_exact(pre_four)
    return (pre_one, pre_two, act_two, pre_three, pre_four, act_four)

def lpips_layer(feat_dec, feat_tgt, lin, count):
    norm_dec = jnp.sqrt(lax.optimization_barrier(jnp.sum(feat_dec * feat_dec, 1, keepdims=True)) + 1e-06)
    norm_tgt = jnp.sqrt(lax.optimization_barrier(jnp.sum(feat_tgt * feat_tgt, 1, keepdims=True)) + 1e-06)
    unit_dec = feat_dec / norm_dec
    differ = unit_dec - feat_tgt / norm_tgt
    scaled = lin[None, :, None, None]
    part = jnp.sum(scaled * differ * differ) / count
    grad_unit = 2.0 * scaled * differ / count
    grad_feat = (grad_unit - unit_dec * lax.optimization_barrier(jnp.sum(grad_unit * unit_dec, 1, keepdims=True))) / norm_dec
    return (part, grad_feat)

def one_frame(pair, out_weight, out_bias, weights, lin_one, lin_two):
    features = pair[0][None]
    targets = pair[1][None]
    weight_one, bias_one, weight_two, bias_two, weight_three, bias_three, weight_four, bias_four = weights
    height = features.shape[2]
    width = features.shape[3]
    feat_pad = pad_rows(features)
    decoded = (conv_valid(feat_pad, out_weight) + out_bias[None, :, None, None]).astype(jnp.bfloat16)
    image_dec = ((decoded.astype(jnp.float32) - shift_array()) / scale_array()).astype(jnp.bfloat16)
    image_tgt = ((targets.astype(jnp.float32) - shift_array()) / scale_array()).astype(jnp.bfloat16)
    pre_one, pre_two, act_two, pre_three, pre_four, act_four = vgg_forward(image_dec, weights)
    tgt_acts = vgg_forward(image_tgt, weights)
    part_one, grad_two = lpips_layer(act_two, tgt_acts[2], lin_one, float(height * width))
    part_two, grad_four = lpips_layer(act_four, tgt_acts[5], lin_two, float(height // 2 * (width // 2)))
    grad_pre4 = (grad_four * gelu_slope(pre_four)).astype(jnp.bfloat16)
    grad_act3 = conv_valid(pad_rows(grad_pre4), flipped(weight_four))
    grad_pre3 = (grad_act3 * gelu_slope(pre_three)).astype(jnp.bfloat16)
    grad_pool = conv_valid(pad_rows(grad_pre3), flipped(weight_three))
    grad_pre2 = ((grad_two + 0.25 * upsample(grad_pool)) * gelu_slope(pre_two)).astype(jnp.bfloat16)
    grad_act1 = conv_valid(pad_rows(grad_pre2), flipped(weight_two))
    grad_pre1 = (grad_act1 * gelu_slope(pre_one)).astype(jnp.bfloat16)
    grad_image = conv_valid(pad_rows(grad_pre1), flipped(weight_one))
    grad_dec = (grad_image / scale_array()).astype(jnp.bfloat16)
    feature_grad = conv_valid(pad_rows(grad_dec), flipped(out_weight)).astype(jnp.bfloat16)
    weight_grad = grad_from_input(grad_dec, feat_pad)
    bias_grad = lax.optimization_barrier(jnp.sum(grad_dec.astype(jnp.float32), (0, 2, 3)))
    return (part_one + part_two, feature_grad[0], weight_grad, bias_grad)

def reference(features, out_weight, out_bias, targets, weight_one, bias_one, weight_two, bias_two, weight_three, bias_three, weight_four, bias_four, lin_one, lin_two):
    weights = (weight_one, bias_one, weight_two, bias_two, weight_three, bias_three, weight_four, bias_four)

    def runner(pair):
        return one_frame(pair, out_weight, out_bias, weights, lin_one, lin_two)
    parts, feature_grad, weight_grads, bias_grads = lax.map(runner, (features, targets))
    return (jnp.sum(parts), feature_grad, lax.optimization_barrier(jnp.sum(weight_grads, 0)), lax.optimization_barrier(jnp.sum(bias_grads, 0)))
```

```python
import math

import jax
import jax.numpy as jnp
from jax import lax
from jax.experimental import pallas as pl
from jax.experimental.pallas import tpu as pltpu
from jax.sharding import PartitionSpec as P

shift_values = [-0.03, -0.088, -0.188]
scale_values = [0.458, 0.448, 0.45]
PAD = 8
HALO = 6
F32 = jnp.float32
BF16 = jnp.bfloat16

erf_top = [0.00022905065861350646, 0.0034082910107109506, 0.050955695062380861, 0.18520832239976145, 1.128379143519084]
erf_bottom = [-1.1791602954361697e-7, 0.000023547966471313185, 0.0010179625278914885, 0.014070470171167667, 0.11098505178285362, 0.49746925110067538, 1.0]


def poly(x, coefs):
    total = jnp.full_like(x, coefs[0])
    for c in coefs[1:]:
        total = total * x + c
    return total


def phi(v):
    x = jnp.clip(v * (1.0 / math.sqrt(2.0)), -3.832506856900711, 3.832506856900711)
    sq = x * x
    return 0.5 + 0.5 * (x * poly(sq, erf_top) / poly(sq, erf_bottom))


def slope_of(v, cdf):
    return cdf + v * (jnp.exp(-0.5 * v * v) * (1.0 / math.sqrt(2.0 * math.pi)))


def dot(a, b):
    return jnp.dot(a, b, preferred_element_type=F32)


def left_right(x):
    width = x.shape[1]
    col = lax.broadcasted_iota(jnp.int32, x.shape, 1)
    left = jnp.where(col == 0, 0.0, pltpu.roll(x, 1, 1))
    right = jnp.where(col == width - 1, 0.0, pltpu.roll(x, width - 1, 1))
    return left, right


def put_taps(ref, where, x):
    c = x.shape[0]
    left, right = left_right(x)
    if c % 16:
        ref[where] = jnp.concatenate([left, x, right], 0).astype(BF16)
    else:
        ref[where + (slice(0, c),)] = left.astype(BF16)
        ref[where + (slice(c, 2 * c),)] = x.astype(BF16)
        ref[where + (slice(2 * c, 3 * c),)] = right.astype(BF16)


def fold_taps(y):
    n = y.shape[0] // 3
    width = y.shape[1]
    col = lax.broadcasted_iota(jnp.int32, (n, width), 1)
    left = jnp.where(col == 0, 0.0, pltpu.roll(y[:n], 1, 1))
    right = jnp.where(col == width - 1, 0.0, pltpu.roll(y[2 * n :], width - 1, 1))
    return left + y[n : 2 * n] + right


def conv_row(w_ref, x_ref, where, row):
    total = dot(w_ref[0], x_ref[where + (row,)])
    for a in (1, 2):
        total = total + dot(w_ref[a], x_ref[where + (row + a,)])
    return total


def two_parts(x):
    high = x.astype(BF16)
    low = (x - high.astype(F32)).astype(BF16)
    return high, low


def exact_dot(x, m):
    high, low = two_parts(x)
    return dot(high, m) + dot(low, m)


def lpips(dec, tgt, lin, count):
    inv_dec = 1.0 / jnp.sqrt(jnp.sum(dec * dec, 0, keepdims=True) + 1e-06)
    inv_tgt = 1.0 / jnp.sqrt(jnp.sum(tgt * tgt, 0, keepdims=True) + 1e-06)
    unit = dec * inv_dec
    differ = unit - tgt * inv_tgt
    weighted = lin * differ
    part = jnp.sum(weighted * differ, 0, keepdims=True) * (1.0 / count)
    grad = weighted * (2.0 / count)
    along = jnp.sum(grad * unit, 0, keepdims=True)
    return part, (grad - unit * along) * inv_dec


def channel_consts():
    o = lax.broadcasted_iota(jnp.int32, (PAD, 1), 0)

    def pick(values, other):
        out = jnp.full((PAD, 1), other, F32)
        for i, v in enumerate(values):
            out = jnp.where(o == i, v, out)
        return out

    return o, pick(shift_values, 0.0), pick(scale_values, 1.0)


def out_conv_kernel(f_ref, w_ref, own_ref, top_ref, bottom_ref):
    rows = f_ref.shape[0]
    width = f_ref.shape[2]
    folded = [fold_taps(dot(w_ref[...], f_ref[s])) for s in range(rows)]
    out = []
    for t in range(rows + 2):
        total = jnp.zeros((PAD, width), F32)
        for a in range(3):
            s = t + a - 2
            if 0 <= s < rows:
                total = total + folded[s][a * PAD : (a + 1) * PAD]
        out.append(total)
        own_ref[t] = total
    for k in range(HALO + 1):
        top_ref[k] = out[k]
        bottom_ref[k] = out[rows + 2 - (HALO + 1) + k]


def forward_kernel(
    start_ref, prev_ref, own_ref, next_ref, tprev_ref, town_ref, tnext_ref, ob_ref,
    w1_ref, b1_ref, w2_ref, b2_ref, w3_ref, b3_ref, w4_ref, b4_ref, l1_ref, l2_ref, pool_ref,
    s1_ref, gf_ref, s2_ref, s3_ref, g4_ref, loss_ref,
    x1, x2, x3, x4, part1, part2, *, height,
):
    rows = town_ref.shape[0]
    width = town_ref.shape[2]
    start = start_ref[0]
    o, shift, scale = channel_consts()

    def image(v, row):
        im = ((v.astype(BF16).astype(F32) - shift) / scale).astype(BF16).astype(F32)
        inside = jnp.logical_and(row >= 0, row < height)
        return jnp.where(jnp.logical_and(o < 3, inside), im, 0.0)

    for e in range(rows + 2 * HALO):
        v = jnp.zeros((PAD, width), F32)
        if HALO - 1 <= e < HALO + rows + 1:
            v = v + own_ref[e - HALO + 1]
        if e < HALO + 1:
            v = v + prev_ref[e]
        if e >= HALO + rows - 1:
            v = v + next_ref[e - (HALO + rows - 1)]
        put_taps(x1, (0, e), image(v + ob_ref[...], start + e - HALO))
        if e < HALO:
            tv = tprev_ref[e]
        elif e < HALO + rows:
            tv = town_ref[e - HALO]
        else:
            tv = tnext_ref[e - HALO - rows]
        put_taps(x1, (1, e), image(tv.astype(F32), start + e - HALO))

    def layer_one(q, carry):
        row = start + q - (HALO - 1)
        inside = jnp.logical_and(row >= 0, row < height)
        for im in range(2):
            pre = conv_row(w1_ref, x1, (im,), q) + b1_ref[...]
            cdf = phi(pre)
            put_taps(x2, (im, q), jnp.where(inside, pre * cdf, 0.0))
            if im == 0:
                s1_ref[q] = slope_of(pre, cdf)
        return carry

    lax.fori_loop(0, rows + 2 * HALO - 2, layer_one, 0)

    part1[...] = jnp.zeros_like(part1)
    part2[...] = jnp.zeros_like(part2)
    half = rows // 2
    edge = HALO - 4

    def layer_two(p, carry):
        row = start // 2 + p - edge
        inside = jnp.logical_and(row >= 0, row < height // 2)
        pres = [[conv_row(w2_ref, x2, (im,), 2 * p + k) + b2_ref[...] for k in range(2)] for im in range(2)]
        cdfs = [[phi(pres[im][k]) for k in range(2)] for im in range(2)]
        acts = [[pres[im][k] * cdfs[im][k] for k in range(2)] for im in range(2)]
        for im in range(2):
            pooled = exact_dot(acts[im][0] + acts[im][1], pool_ref[...])
            put_taps(x3, (im, p), jnp.where(inside, pooled, 0.0))

        @pl.when(jnp.logical_and(p >= edge, p < edge + half))
        def _():
            for k in range(2):
                part, grad = lpips(acts[0][k], acts[1][k], l1_ref[...], float(height * width))
                part1[...] += part
                gf_ref[2 * (p - edge) + k] = grad
                s2_ref[2 * (p - edge) + k] = slope_of(pres[0][k], cdfs[0][k])

        return carry

    lax.fori_loop(0, half + 2 * edge, layer_two, 0)

    def layer_three(t, carry):
        row = start // 2 + t - (edge - 1)
        inside = jnp.logical_and(row >= 0, row < height // 2)
        for im in range(2):
            pre = conv_row(w3_ref, x3, (im,), t) + b3_ref[...]
            cdf = phi(pre)
            put_taps(x4, (im, t), jnp.where(inside, pre * cdf, 0.0))
            if im == 0:
                s3_ref[t] = jnp.where(inside, slope_of(pre, cdf), 0.0)
        return carry

    lax.fori_loop(0, half + 2, layer_three, 0)

    def layer_four(u, carry):
        pres = [conv_row(w4_ref, x4, (im,), u) + b4_ref[...] for im in range(2)]
        cdfs = [phi(v) for v in pres]
        part, grad = lpips(
            pres[0] * cdfs[0], pres[1] * cdfs[1], l2_ref[...], float(height // 2 * (width // 2))
        )
        part2[...] += part
        g4_ref[u] = (grad * slope_of(pres[0], cdfs[0])).astype(BF16)
        return carry

    lax.fori_loop(0, half, layer_four, 0)
    loss_ref[...] = jnp.sum(part1[...], 1, keepdims=True) + jnp.sum(part2[...], 1, keepdims=True)


def deep_back_kernel(
    prev_ref, own_ref, next_ref, s3_ref, gf_ref, s2_ref, w4_ref, w3_ref, up_ref, g2_ref, x5, x6
):
    half = own_ref.shape[0]
    for e in range(half + 4):
        if e < 2:
            v = prev_ref[e]
        elif e < half + 2:
            v = own_ref[e - 2]
        else:
            v = next_ref[e - half - 2]
        put_taps(x5, (e,), v.astype(F32))

    def third(t, carry):
        put_taps(x6, (t,), conv_row(w4_ref, x5, (), t) * s3_ref[t])
        return carry

    lax.fori_loop(0, half + 2, third, 0)

    def second(p, carry):
        wide = exact_dot(conv_row(w3_ref, x6, (), p), up_ref[...])
        for k in range(2):
            g2_ref[2 * p + k] = ((gf_ref[2 * p + k] + wide) * s2_ref[2 * p + k]).astype(BF16)
        return carry

    lax.fori_loop(0, half, second, 0)


def shallow_back_kernel(
    start_ref, prev_ref, own_ref, next_ref, s1_ref, w2_ref, w1_ref, f_ref, loss_ref,
    taps_ref, sums_ref, x7, y, *, height,
):
    rows = own_ref.shape[0]
    start = start_ref[0]
    o, shift, scale = channel_consts()
    for e in range(rows + 6):
        if e < 3:
            v = prev_ref[e]
        elif e < rows + 3:
            v = own_ref[e - 3]
        else:
            v = next_ref[e - rows - 3]
        put_taps(x7, (e,), v.astype(F32))

    def first(q, carry):
        row = start + q - 2
        inside = jnp.logical_and(row >= 0, row < height)
        g1 = conv_row(w2_ref, x7, (), q) * s1_ref[q + HALO - 3]
        g1 = jnp.where(inside, g1, 0.0).astype(BF16)
        y[q] = fold_taps(dot(w1_ref[...], g1))
        return carry

    lax.fori_loop(0, rows + 4, first, 0)
    bias = jnp.zeros((PAD, 1), F32)
    for p in range(rows + 2):
        row = start + p - 1
        inside = jnp.logical_and(row >= 0, row < height)
        g = y[p, 0:PAD] + y[p + 1, PAD : 2 * PAD] + y[p + 2, 2 * PAD : 3 * PAD]
        g = jnp.where(inside, (g / scale).astype(BF16).astype(F32), 0.0)
        if 1 <= p <= rows:
            bias = bias + jnp.sum(g, 1, keepdims=True)
        put_taps(taps_ref, (p,), g)
    cf = f_ref.shape[1]
    for a in range(3):
        total = jnp.zeros((3 * PAD, cf), F32)
        for s in range(rows):
            total = total + lax.dot_general(
                taps_ref[s + 2 - a], f_ref[s], (((1,), (1,)), ((), ())), preferred_element_type=F32
            )
        sums_ref[a] = total
    last = jnp.where(o == 3, loss_ref[...], bias)
    sums_ref[3] = jnp.zeros((3 * PAD, cf), F32)
    sums_ref[3, 0:PAD] = jnp.broadcast_to(last, (PAD, cf))


def feature_kernel(taps_ref, w_ref, out_ref):
    for r in range(out_ref.shape[0]):
        out_ref[r] = conv_row(w_ref, taps_ref, (), r).astype(BF16)


def call(kernel, n_in, outs, scratch=(), smem=()):
    return pl.pallas_call(
        kernel,
        in_specs=[
            pl.BlockSpec(memory_space=pltpu.SMEM if i in smem else pltpu.VMEM) for i in range(n_in)
        ],
        out_specs=[pl.BlockSpec(memory_space=pltpu.VMEM) for _ in outs],
        out_shape=[jax.ShapeDtypeStruct(s, t) for s, t in outs],
        scratch_shapes=[pltpu.VMEM(s, t) for s, t in scratch],
        compiler_params=pltpu.CompilerParams(vmem_limit_bytes=48 * 1024 * 1024),
    )


def flipped(weight):
    return jnp.flip(weight, (2, 3)).transpose(1, 0, 2, 3)


def taps_in(w, pad=0):
    o, i = w.shape[:2]
    w = jnp.pad(w, ((0, 0), (0, pad), (0, 0), (0, 0)))
    return w.transpose(2, 0, 3, 1).reshape(3, o, 3 * (i + pad))


def taps_out(w):
    o, i = w.shape[:2]
    w = jnp.pad(w, ((0, PAD - o), (0, 0), (0, 0), (0, 0)))
    return w.transpose(3, 2, 0, 1).reshape(9 * PAD, i)


def from_neighbours(last, first):
    size = lax.axis_size("row")
    up = [(i, i + 1) for i in range(size - 1)]
    down = [(i + 1, i) for i in range(size - 1)]
    return lax.ppermute(last, "row", up), lax.ppermute(first, "row", down)


def local(
    features, out_weight, out_bias, targets, weight_one, bias_one, weight_two, bias_two,
    weight_three, bias_three, weight_four, bias_four, lin_one, lin_two,
):
    frames, cf, rows, width = features.shape
    c1 = weight_one.shape[0]
    c2 = weight_three.shape[0]
    assert frames == 1 and rows % 2 == 0 and rows > HALO
    height = rows * lax.axis_size("row")
    half, wh = rows // 2, width // 2
    edge = HALO - 4
    start = (lax.axis_index("row") * rows).astype(jnp.int32).reshape(1)

    tgt = jnp.pad(targets[0].transpose(1, 0, 2), ((0, 0), (0, PAD - targets.shape[1]), (0, 0)))
    tprev, tnext = from_neighbours(tgt[rows - HALO :], tgt[:HALO])
    feat = features[0].transpose(1, 0, 2)
    band = (HALO + 1, PAD, width)
    own, top, bottom = call(
        out_conv_kernel, 2, [((rows + 2, PAD, width), F32), (band, F32), (band, F32)]
    )(feat, taps_out(out_weight))
    prev, nxt = from_neighbours(bottom, top)

    j = jnp.arange(width)[:, None] // 2 == jnp.arange(wh)[None, :]
    pool = jnp.where(j, 0.25, 0.0).astype(BF16)
    col = lambda b: b[:, None]
    ob = jnp.pad(out_bias, (0, PAD - out_bias.shape[0]))

    r1 = rows + 2 * HALO
    s1, gf, s2, s3, g4, loss = call(
        lambda *r: forward_kernel(*r, height=height), 19,
        [
            ((r1 - 2, c1, width), F32), ((rows, c1, width), F32), ((rows, c1, width), F32),
            ((half + 2, c2, wh), F32), ((half, c2, wh), BF16), ((1, 1), F32),
        ],
        [
            ((2, r1, 3 * PAD, width), BF16), ((2, r1 - 2, 3 * c1, width), BF16),
            ((2, half + 2 * edge, 3 * c1, wh), BF16), ((2, half + 2, 3 * c2, wh), BF16),
            ((1, width), F32), ((1, wh), F32),
        ],
        smem=(0,),
    )(
        start, prev, own, nxt, tprev, tgt, tnext, col(ob),
        taps_in(weight_one, PAD - weight_one.shape[1]), col(bias_one), taps_in(weight_two), col(bias_two),
        taps_in(weight_three), col(bias_three), taps_in(weight_four), col(bias_four),
        col(lin_one), col(lin_two), pool,
    )

    gprev, gnext = from_neighbours(g4[half - 2 :], g4[:2])
    (g2,) = call(
        deep_back_kernel, 9, [((rows, c1, width), BF16)],
        [((half + 4, 3 * c2, wh), BF16), ((half + 2, 3 * c2, wh), BF16)],
    )(gprev, g4, gnext, s3, gf, s2, taps_in(flipped(weight_four)), taps_in(flipped(weight_three)), pool.T)

    g2prev, g2next = from_neighbours(g2[rows - 3 :], g2[:3])
    taps, sums = call(
        lambda *r: shallow_back_kernel(*r, height=height), 9,
        [((rows + 2, 3 * PAD, width), BF16), ((4, 3 * PAD, cf), F32)],
        [((rows + 6, 3 * c1, width), BF16), ((rows + 4, 3 * PAD, width), F32)],
        smem=(0,),
    )(start, g2prev, g2, g2next, s1, taps_in(flipped(weight_two)), taps_out(flipped(weight_one)), feat, loss)
    sums = lax.psum(sums, ("clip", "row"))
    (fg,) = call(feature_kernel, 2, [((rows, cf, width), BF16)])(
        taps, taps_in(flipped(out_weight), PAD - out_weight.shape[0])
    )
    feature_grad = fg.transpose(1, 0, 2)[None]
    wg = sums[:3].reshape(3, 3, PAD, cf)[:, ::-1, : out_weight.shape[0]].transpose(2, 3, 0, 1)
    return (sums[3, 3, 0], feature_grad, wg, sums[3, : out_weight.shape[0], 0])


def solution(mesh):
    tile = P("clip", None, "row", None)
    return jax.shard_map(
        local,
        mesh=mesh,
        in_specs=(tile, P(), P(), tile) + (P(),) * 10,
        out_specs=(P(), tile, P(), P()),
        check_vma=False,
    )
```

```python
import math

import jax
import jax.numpy as jnp
from jax import lax
from jax.experimental import pallas as pl
from jax.experimental.pallas import tpu as pltpu
from jax.sharding import PartitionSpec as P

shift_values = [-0.03, -0.088, -0.188]
scale_values = [0.458, 0.448, 0.45]
PAD = 8
TGT = 4
HALO = 6
F32 = jnp.float32
BF16 = jnp.bfloat16

erf_top = [0.00022905065861350646, 0.0034082910107109506, 0.050955695062380861, 0.18520832239976145, 1.128379143519084]
erf_bottom = [-1.1791602954361697e-7, 0.000023547966471313185, 0.0010179625278914885, 0.014070470171167667, 0.11098505178285362, 0.49746925110067538, 1.0]


def poly(x, coefs):
    total = jnp.full_like(x, coefs[0])
    for c in coefs[1:]:
        total = total * x + c
    return total


def phi(v):
    x = jnp.clip(v * (1.0 / math.sqrt(2.0)), -3.832506856900711, 3.832506856900711)
    sq = x * x
    return 0.5 + 0.5 * (x * poly(sq, erf_top) / poly(sq, erf_bottom))


def slope_of(v, cdf):
    return cdf + v * (jnp.exp(-0.5 * v * v) * (1.0 / math.sqrt(2.0 * math.pi)))


def dot(a, b):
    return jnp.dot(a, b, preferred_element_type=F32)


def left_right(x):
    width = x.shape[1]
    col = lax.broadcasted_iota(jnp.int32, x.shape, 1)
    left = jnp.where(col == 0, 0.0, pltpu.roll(x, 1, 1))
    right = jnp.where(col == width - 1, 0.0, pltpu.roll(x, width - 1, 1))
    return left, right


def put_taps(ref, where, x):
    c = x.shape[0]
    left, right = left_right(x)
    if c % 16:
        ref[where] = jnp.concatenate([left, x, right], 0).astype(BF16)
    else:
        ref[where + (slice(0, c),)] = left.astype(BF16)
        ref[where + (slice(c, 2 * c),)] = x.astype(BF16)
        ref[where + (slice(2 * c, 3 * c),)] = right.astype(BF16)


def fold_taps(y):
    n = y.shape[0] // 3
    width = y.shape[1]
    col = lax.broadcasted_iota(jnp.int32, (n, width), 1)
    left = jnp.where(col == 0, 0.0, pltpu.roll(y[:n], 1, 1))
    right = jnp.where(col == width - 1, 0.0, pltpu.roll(y[2 * n :], width - 1, 1))
    return left + y[n : 2 * n] + right


def conv_row(w_ref, x_ref, where, row):
    total = dot(w_ref[0], x_ref[where + (row,)])
    for a in (1, 2):
        total = total + dot(w_ref[a], x_ref[where + (row + a,)])
    return total


def two_parts(x):
    high = x.astype(BF16)
    low = (x - high.astype(F32)).astype(BF16)
    return high, low


def exact_dot(x, m):
    high, low = two_parts(x)
    return dot(high, m) + dot(low, m)


def lpips(dec, tgt, lin, count):
    inv_dec = 1.0 / jnp.sqrt(jnp.sum(dec * dec, 0, keepdims=True) + 1e-06)
    inv_tgt = 1.0 / jnp.sqrt(jnp.sum(tgt * tgt, 0, keepdims=True) + 1e-06)
    unit = dec * inv_dec
    differ = unit - tgt * inv_tgt
    weighted = lin * differ
    part = jnp.sum(weighted * differ, 0, keepdims=True) * (1.0 / count)
    grad = weighted * (2.0 / count)
    along = jnp.sum(grad * unit, 0, keepdims=True)
    return part, (grad - unit * along) * inv_dec


def channel_consts():
    o = lax.broadcasted_iota(jnp.int32, (PAD, 1), 0)

    def pick(values, other):
        out = jnp.full((PAD, 1), other, F32)
        for i, v in enumerate(values):
            out = jnp.where(o % TGT == i, v, out)
        return out

    return o, pick(shift_values, 0.0), pick(scale_values, 1.0)


def out_conv_kernel(f_ref, w_ref, t_ref, own_ref, top_ref, bottom_ref):
    rows = f_ref.shape[0]
    width = f_ref.shape[2]
    folded = [fold_taps(dot(w_ref[...], f_ref[s])) for s in range(rows)]
    out = []
    for t in range(rows + 2):
        total = jnp.zeros((PAD, width), F32)
        for a in range(3):
            s = t + a - 2
            if 0 <= s < rows:
                total = total + folded[s][a * PAD : (a + 1) * PAD]
        if 1 <= t <= rows:
            total = total + t_ref[t - 1]
        out.append(total)
        own_ref[t] = total
    for k in range(HALO + 1):
        top_ref[k] = out[k]
        bottom_ref[k] = out[rows + 2 - (HALO + 1) + k]


def forward_kernel(
    start_ref, prev_ref, own_ref, next_ref, ob_ref,
    w1_ref, b1_ref, w2_ref, b2_ref, w3_ref, b3_ref, w4_ref, b4_ref, l1_ref, l2_ref, pool_ref,
    s1_ref, gf_ref, s2_ref, s3_ref, g4_ref, loss_ref,
    x1, x2, x3, x4, part1, part2, *, height,
):
    rows = own_ref.shape[0] - 2
    width = own_ref.shape[2]
    start = start_ref[0]
    o, shift, scale = channel_consts()

    def image(v, row):
        im = ((v.astype(BF16).astype(F32) - shift) / scale).astype(BF16).astype(F32)
        inside = jnp.logical_and(row >= 0, row < height)
        return jnp.where(jnp.logical_and(o % TGT < 3, inside), im, 0.0)

    for e in range(rows + 2 * HALO):
        v = jnp.zeros((PAD, width), F32)
        if HALO - 1 <= e < HALO + rows + 1:
            v = v + own_ref[e - HALO + 1]
        if e < HALO + 1:
            v = v + prev_ref[e]
        if e >= HALO + rows - 1:
            v = v + next_ref[e - (HALO + rows - 1)]
        put_taps(x1, (e,), image(v + ob_ref[...], start + e - HALO))

    def layer_one(q, carry):
        row = start + q - (HALO - 1)
        inside = jnp.logical_and(row >= 0, row < height)
        both = conv_row(w1_ref, x1, (), q)
        c1 = b1_ref.shape[0]
        for im in range(2):
            pre = both[im * c1 : (im + 1) * c1] + b1_ref[...]
            cdf = phi(pre)
            put_taps(x2, (im, q), jnp.where(inside, pre * cdf, 0.0))
            if im == 0:
                s1_ref[q] = slope_of(pre, cdf)
        return carry

    lax.fori_loop(0, rows + 2 * HALO - 2, layer_one, 0)

    part1[...] = jnp.zeros_like(part1)
    part2[...] = jnp.zeros_like(part2)
    half = rows // 2
    edge = HALO - 4

    def layer_two(p, carry):
        row = start // 2 + p - edge
        inside = jnp.logical_and(row >= 0, row < height // 2)
        pres = [[conv_row(w2_ref, x2, (im,), 2 * p + k) + b2_ref[...] for k in range(2)] for im in range(2)]
        cdfs = [[phi(pres[im][k]) for k in range(2)] for im in range(2)]
        acts = [[pres[im][k] * cdfs[im][k] for k in range(2)] for im in range(2)]
        for im in range(2):
            pooled = exact_dot(acts[im][0] + acts[im][1], pool_ref[...])
            put_taps(x3, (im, p), jnp.where(inside, pooled, 0.0))

        @pl.when(jnp.logical_and(p >= edge, p < edge + half))
        def _():
            for k in range(2):
                part, grad = lpips(acts[0][k], acts[1][k], l1_ref[...], float(height * width))
                part1[...] += part
                gf_ref[2 * (p - edge) + k] = grad
                s2_ref[2 * (p - edge) + k] = slope_of(pres[0][k], cdfs[0][k])

        return carry

    lax.fori_loop(0, half + 2 * edge, layer_two, 0)

    def layer_three(t, carry):
        row = start // 2 + t - (edge - 1)
        inside = jnp.logical_and(row >= 0, row < height // 2)
        for im in range(2):
            pre = conv_row(w3_ref, x3, (im,), t) + b3_ref[...]
            cdf = phi(pre)
            put_taps(x4, (im, t), jnp.where(inside, pre * cdf, 0.0))
            if im == 0:
                s3_ref[t] = jnp.where(inside, slope_of(pre, cdf), 0.0)
        return carry

    lax.fori_loop(0, half + 2, layer_three, 0)

    def layer_four(u, carry):
        pres = [conv_row(w4_ref, x4, (im,), u) + b4_ref[...] for im in range(2)]
        cdfs = [phi(v) for v in pres]
        part, grad = lpips(
            pres[0] * cdfs[0], pres[1] * cdfs[1], l2_ref[...], float(height // 2 * (width // 2))
        )
        part2[...] += part
        g4_ref[u] = (grad * slope_of(pres[0], cdfs[0])).astype(BF16)
        return carry

    lax.fori_loop(0, half, layer_four, 0)
    loss_ref[...] = jnp.sum(part1[...], 1, keepdims=True) + jnp.sum(part2[...], 1, keepdims=True)


def deep_back_kernel(
    prev_ref, own_ref, next_ref, s3_ref, gf_ref, s2_ref, w4_ref, w3_ref, up_ref, g2_ref, x5, x6
):
    half = own_ref.shape[0]
    for e in range(half + 4):
        if e < 2:
            v = prev_ref[e]
        elif e < half + 2:
            v = own_ref[e - 2]
        else:
            v = next_ref[e - half - 2]
        put_taps(x5, (e,), v.astype(F32))

    def third(t, carry):
        put_taps(x6, (t,), conv_row(w4_ref, x5, (), t) * s3_ref[t])
        return carry

    lax.fori_loop(0, half + 2, third, 0)

    def second(p, carry):
        wide = exact_dot(conv_row(w3_ref, x6, (), p), up_ref[...])
        for k in range(2):
            g2_ref[2 * p + k] = ((gf_ref[2 * p + k] + wide) * s2_ref[2 * p + k]).astype(BF16)
        return carry

    lax.fori_loop(0, half, second, 0)


def shallow_back_kernel(
    start_ref, prev_ref, own_ref, next_ref, s1_ref, w2_ref, w1_ref, f_ref, loss_ref,
    taps_ref, sums_ref, x7, y, *, height,
):
    rows = own_ref.shape[0]
    start = start_ref[0]
    o, shift, scale = channel_consts()
    for e in range(rows + 6):
        if e < 3:
            v = prev_ref[e]
        elif e < rows + 3:
            v = own_ref[e - 3]
        else:
            v = next_ref[e - rows - 3]
        put_taps(x7, (e,), v.astype(F32))

    def first(q, carry):
        row = start + q - 2
        inside = jnp.logical_and(row >= 0, row < height)
        g1 = conv_row(w2_ref, x7, (), q) * s1_ref[q + HALO - 3]
        g1 = jnp.where(inside, g1, 0.0).astype(BF16)
        y[q] = fold_taps(dot(w1_ref[...], g1))
        return carry

    lax.fori_loop(0, rows + 4, first, 0)
    bias = jnp.zeros((PAD, 1), F32)
    for p in range(rows + 2):
        row = start + p - 1
        inside = jnp.logical_and(row >= 0, row < height)
        g = y[p, 0:PAD] + y[p + 1, PAD : 2 * PAD] + y[p + 2, 2 * PAD : 3 * PAD]
        g = jnp.where(inside, (g / scale).astype(BF16).astype(F32), 0.0)
        if 1 <= p <= rows:
            bias = bias + jnp.sum(g, 1, keepdims=True)
        put_taps(taps_ref, (p,), g)
    cf = f_ref.shape[1]
    totals = []
    for a in range(3):
        total = jnp.zeros((3 * PAD, cf), F32)
        for s in range(rows):
            total = total + lax.dot_general(
                taps_ref[s + 2 - a], f_ref[s], (((1,), (1,)), ((), ())), preferred_element_type=F32
            )
        totals.append(total)
    last = jnp.where(o == 7, loss_ref[...], pltpu.roll(jnp.broadcast_to(bias, (PAD, cf)), TGT, 0))
    sums_ref[0] = totals[0] + pltpu.roll(totals[1], TGT, 0)
    sums_ref[1] = totals[2]
    sums_ref[1, 0:PAD] = totals[2][0:PAD] + last


def feature_kernel(taps_ref, w_ref, out_ref):
    for r in range(out_ref.shape[0]):
        out_ref[r] = conv_row(w_ref, taps_ref, (), r).astype(BF16)


def call(kernel, n_in, outs, scratch=(), smem=()):
    return pl.pallas_call(
        kernel,
        in_specs=[
            pl.BlockSpec(memory_space=pltpu.SMEM if i in smem else pltpu.VMEM) for i in range(n_in)
        ],
        out_specs=[pl.BlockSpec(memory_space=pltpu.VMEM) for _ in outs],
        out_shape=[jax.ShapeDtypeStruct(s, t) for s, t in outs],
        scratch_shapes=[pltpu.VMEM(s, t) for s, t in scratch],
        compiler_params=pltpu.CompilerParams(vmem_limit_bytes=48 * 1024 * 1024),
    )


def flipped(weight):
    return jnp.flip(weight, (2, 3)).transpose(1, 0, 2, 3)


def taps_in(w, pad=0):
    o, i = w.shape[:2]
    w = jnp.pad(w, ((0, 0), (0, pad), (0, 0), (0, 0)))
    return w.transpose(2, 0, 3, 1).reshape(3, o, 3 * (i + pad))


def taps_out(w):
    o, i = w.shape[:2]
    w = jnp.pad(w, ((0, PAD - o), (0, 0), (0, 0), (0, 0)))
    return w.transpose(3, 2, 0, 1).reshape(9 * PAD, i)


def summed(array, axis):
    size = lax.axis_size(axis)
    if size & (size - 1):
        return lax.psum(array, axis)
    step = 1
    while step < size:
        array = array + lax.ppermute(array, axis, [(i, i ^ step) for i in range(size)])
        step *= 2
    return array


def from_neighbours(last, first):
    size = lax.axis_size("row")
    up = [(i, i + 1) for i in range(size - 1)]
    down = [(i + 1, i) for i in range(size - 1)]
    return lax.ppermute(last, "row", up), lax.ppermute(first, "row", down)


def local(
    features, out_weight, out_bias, targets, weight_one, bias_one, weight_two, bias_two,
    weight_three, bias_three, weight_four, bias_four, lin_one, lin_two,
):
    frames, cf, rows, width = features.shape
    c1 = weight_one.shape[0]
    c2 = weight_three.shape[0]
    assert frames == 1 and rows % 2 == 0 and rows > HALO
    height = rows * lax.axis_size("row")
    half, wh = rows // 2, width // 2
    edge = HALO - 4
    start = (lax.axis_index("row") * rows).astype(jnp.int32).reshape(1)

    colors = targets.shape[1]
    tgt = targets[0].astype(F32).transpose(1, 0, 2)
    tgt = jnp.pad(tgt, ((0, 0), (TGT, PAD - TGT - colors), (0, 0)))
    feat = features[0].transpose(1, 0, 2)
    band = (HALO + 1, PAD, width)
    own, top, bottom = call(
        out_conv_kernel, 3, [((rows + 2, PAD, width), F32), (band, F32), (band, F32)]
    )(feat, taps_out(out_weight), tgt)
    prev, nxt = from_neighbours(bottom, top)

    j = jnp.arange(width)[:, None] // 2 == jnp.arange(wh)[None, :]
    pool = jnp.where(j, 0.25, 0.0).astype(BF16)
    col = lambda b: b[:, None]
    ob = jnp.pad(out_bias, (0, PAD - out_bias.shape[0]))

    w1 = jnp.pad(weight_one, ((0, 0), (0, PAD - colors), (0, 0), (0, 0)))
    w1 = taps_in(jnp.concatenate([w1, jnp.roll(w1, TGT, 1)], 0))
    r1 = rows + 2 * HALO
    s1, gf, s2, s3, g4, loss = call(
        lambda *r: forward_kernel(*r, height=height), 16,
        [
            ((r1 - 2, c1, width), F32), ((rows, c1, width), F32), ((rows, c1, width), F32),
            ((half + 2, c2, wh), F32), ((half, c2, wh), BF16), ((1, 1), F32),
        ],
        [
            ((r1, 3 * PAD, width), BF16), ((2, r1 - 2, 3 * c1, width), BF16),
            ((2, half + 2 * edge, 3 * c1, wh), BF16), ((2, half + 2, 3 * c2, wh), BF16),
            ((1, width), F32), ((1, wh), F32),
        ],
        smem=(0,),
    )(
        start, prev, own, nxt, col(ob),
        w1, col(bias_one), taps_in(weight_two), col(bias_two),
        taps_in(weight_three), col(bias_three), taps_in(weight_four), col(bias_four),
        col(lin_one), col(lin_two), pool,
    )

    gprev, gnext = from_neighbours(g4[half - 2 :], g4[:2])
    (g2,) = call(
        deep_back_kernel, 9, [((rows, c1, width), BF16)],
        [((half + 4, 3 * c2, wh), BF16), ((half + 2, 3 * c2, wh), BF16)],
    )(gprev, g4, gnext, s3, gf, s2, taps_in(flipped(weight_four)), taps_in(flipped(weight_three)), pool.T)

    g2prev, g2next = from_neighbours(g2[rows - 3 :], g2[:3])
    taps, sums = call(
        lambda *r: shallow_back_kernel(*r, height=height), 9,
        [((rows + 2, 3 * PAD, width), BF16), ((2, 3 * PAD, cf), F32)],
        [((rows + 6, 3 * c1, width), BF16), ((rows + 4, 3 * PAD, width), F32)],
        smem=(0,),
    )(start, g2prev, g2, g2next, s1, taps_in(flipped(weight_two)), taps_out(flipped(weight_one)), feat, loss)
    sums = summed(summed(sums, "row"), "clip")
    (fg,) = call(feature_kernel, 2, [((rows, cf, width), BF16)])(
        taps, taps_in(flipped(out_weight), PAD - out_weight.shape[0])
    )
    feature_grad = fg.transpose(1, 0, 2)[None]
    loss = sums[1, TGT + 3, 0]
    bias_grad = sums[1, TGT : TGT + colors, 0]
    sums = sums.reshape(2, 3, PAD, cf)[:, ::-1]
    wg = jnp.stack([sums[0, :, :colors], sums[0, :, TGT : TGT + colors], sums[1, :, :colors]])
    return (loss, feature_grad, wg.transpose(2, 3, 0, 1), bias_grad)


def solution(mesh):
    tile = P("clip", None, "row", None)
    return jax.shard_map(
        local,
        mesh=mesh,
        in_specs=(tile, P(), P(), tile) + (P(),) * 10,
        out_specs=(P(), tile, P(), P()),
        check_vma=False,
    )
```

```python
import math

import jax
import jax.numpy as jnp
from jax import lax
from jax.experimental import pallas as pl
from jax.experimental.pallas import tpu as pltpu
from jax.sharding import PartitionSpec as P

shift_values = [-0.03, -0.088, -0.188]
scale_values = [0.458, 0.448, 0.45]
PAD = 8
TGT = 4
HALO = 6
F32 = jnp.float32
BF16 = jnp.bfloat16

erf_top = [0.00022905065861350646, 0.0034082910107109506, 0.050955695062380861, 0.18520832239976145, 1.128379143519084]
erf_bottom = [-1.1791602954361697e-7, 0.000023547966471313185, 0.0010179625278914885, 0.014070470171167667, 0.11098505178285362, 0.49746925110067538, 1.0]


def poly(x, coefs):
    total = jnp.full_like(x, coefs[0])
    for c in coefs[1:]:
        total = total * x + c
    return total


LIMIT = 3.832506856900711 * math.sqrt(2.0)
phi_top = [c * 0.5**k * 0.5 * math.sqrt(0.5) for k, c in zip(range(4, -1, -1), erf_top)]
phi_bottom = [c * 0.5**k for k, c in zip(range(6, -1, -1), erf_bottom)]


def phi(v):
    x = jnp.clip(v, -LIMIT, LIMIT)
    sq = x * x
    return 0.5 + x * poly(sq, phi_top) / poly(sq, phi_bottom)


def slope_of(v, cdf):
    return cdf + v * (jnp.exp(-0.5 * v * v) * (1.0 / math.sqrt(2.0 * math.pi)))


def dot(a, b):
    return jnp.dot(a, b, preferred_element_type=F32)


def left_right(x):
    width = x.shape[1]
    col = lax.broadcasted_iota(jnp.int32, x.shape, 1)
    left = jnp.where(col == 0, 0.0, pltpu.roll(x, 1, 1))
    right = jnp.where(col == width - 1, 0.0, pltpu.roll(x, width - 1, 1))
    return left, right


def put_taps(ref, where, x):
    c = x.shape[0]
    left, right = left_right(x)
    if c % 16:
        ref[where] = jnp.concatenate([left, x, right], 0).astype(BF16)
    else:
        ref[where + (slice(0, c),)] = left.astype(BF16)
        ref[where + (slice(c, 2 * c),)] = x.astype(BF16)
        ref[where + (slice(2 * c, 3 * c),)] = right.astype(BF16)


def fold_taps(y):
    n = y.shape[0] // 3
    width = y.shape[1]
    col = lax.broadcasted_iota(jnp.int32, (n, width), 1)
    left = jnp.where(col == 0, 0.0, pltpu.roll(y[:n], 1, 1))
    right = jnp.where(col == width - 1, 0.0, pltpu.roll(y[2 * n :], width - 1, 1))
    return left + y[n : 2 * n] + right


def conv_row(w_ref, x_ref, where, row):
    total = dot(w_ref[0], x_ref[where + (row,)])
    for a in (1, 2):
        total = total + dot(w_ref[a], x_ref[where + (row + a,)])
    return total


def two_parts(x):
    high = x.astype(BF16)
    low = (x - high.astype(F32)).astype(BF16)
    return high, low


def exact_dot(x, m):
    high, low = two_parts(x)
    return dot(high, m) + dot(low, m)


def lpips(dec, tgt, lin, count):
    inv_dec = 1.0 / jnp.sqrt(jnp.sum(dec * dec, 0, keepdims=True) + 1e-06)
    inv_tgt = 1.0 / jnp.sqrt(jnp.sum(tgt * tgt, 0, keepdims=True) + 1e-06)
    unit = dec * inv_dec
    differ = unit - tgt * inv_tgt
    weighted = lin * differ
    part = jnp.sum(weighted * differ, 0, keepdims=True) * (1.0 / count)
    grad = weighted * (2.0 / count)
    along = jnp.sum(grad * unit, 0, keepdims=True)
    return part, (grad - unit * along) * inv_dec


def channel_consts():
    o = lax.broadcasted_iota(jnp.int32, (PAD, 1), 0)

    def pick(values, other):
        out = jnp.full((PAD, 1), other, F32)
        for i, v in enumerate(values):
            out = jnp.where(o % TGT == i, v, out)
        return out

    return o, pick(shift_values, 0.0), pick(scale_values, 1.0)


def out_conv_kernel(f_ref, w_ref, t_ref, own_ref, top_ref, bottom_ref):
    rows = f_ref.shape[0]
    width = f_ref.shape[2]
    folded = [fold_taps(dot(w_ref[...], f_ref[s])) for s in range(rows)]
    out = []
    for t in range(rows + 2):
        total = jnp.zeros((PAD, width), F32)
        for a in range(3):
            s = t + a - 2
            if 0 <= s < rows:
                total = total + folded[s][a * PAD : (a + 1) * PAD]
        if 1 <= t <= rows:
            total = total + t_ref[t - 1]
        out.append(total)
        own_ref[t] = total
    for k in range(HALO + 1):
        top_ref[k] = out[k]
        bottom_ref[k] = out[rows + 2 - (HALO + 1) + k]


def forward_kernel(
    start_ref, prev_ref, own_ref, next_ref, ob_ref,
    w1_ref, b1_ref, w2_ref, b2_ref, w3_ref, b3_ref, w4_ref, b4_ref, l2_ref, pool_ref,
    pre1_ref, cdf1_ref, pre2_ref, cdf2_ref, act2_ref, s3_ref, g4_ref, loss_ref,
    x1, x2, x3, x4, part2, *, height,
):
    rows = own_ref.shape[0] - 2
    width = own_ref.shape[2]
    start = start_ref[0]
    o, shift, scale = channel_consts()

    def image(v, row):
        im = ((v.astype(BF16).astype(F32) - shift) / scale).astype(BF16).astype(F32)
        inside = jnp.logical_and(row >= 0, row < height)
        return jnp.where(jnp.logical_and(o % TGT < 3, inside), im, 0.0)

    for e in range(rows + 2 * HALO):
        v = jnp.zeros((PAD, width), F32)
        if HALO - 1 <= e < HALO + rows + 1:
            v = v + own_ref[e - HALO + 1]
        if e < HALO + 1:
            v = v + prev_ref[e]
        if e >= HALO + rows - 1:
            v = v + next_ref[e - (HALO + rows - 1)]
        put_taps(x1, (e,), image(v + ob_ref[...], start + e - HALO))

    def layer_one(q, carry):
        row = start + q - (HALO - 1)
        inside = jnp.logical_and(row >= 0, row < height)
        both = conv_row(w1_ref, x1, (), q)
        c1 = b1_ref.shape[0]
        for im in range(2):
            pre = both[im * c1 : (im + 1) * c1] + b1_ref[...]
            cdf = phi(pre)
            put_taps(x2, (im, q), jnp.where(inside, pre * cdf, 0.0))
            if im == 0:
                pre1_ref[q] = pre
                cdf1_ref[q] = cdf
        return carry

    lax.fori_loop(0, rows + 2 * HALO - 2, layer_one, 0)

    part2[...] = jnp.zeros_like(part2)
    half = rows // 2
    edge = HALO - 4

    def layer_two(p, carry):
        row = start // 2 + p - edge
        inside = jnp.logical_and(row >= 0, row < height // 2)
        pres = [[conv_row(w2_ref, x2, (im,), 2 * p + k) + b2_ref[...] for k in range(2)] for im in range(2)]
        cdfs = [[phi(pres[im][k]) for k in range(2)] for im in range(2)]
        acts = [[pres[im][k] * cdfs[im][k] for k in range(2)] for im in range(2)]
        for im in range(2):
            pooled = exact_dot(acts[im][0] + acts[im][1], pool_ref[...])
            put_taps(x3, (im, p), jnp.where(inside, pooled, 0.0))

        @pl.when(jnp.logical_and(p >= edge, p < edge + half))
        def _():
            for k in range(2):
                pre2_ref[2 * (p - edge) + k] = pres[0][k]
                cdf2_ref[2 * (p - edge) + k] = cdfs[0][k]
                act2_ref[2 * (p - edge) + k] = acts[1][k]

        return carry

    lax.fori_loop(0, half + 2 * edge, layer_two, 0)

    def layer_three(t, carry):
        row = start // 2 + t - (edge - 1)
        inside = jnp.logical_and(row >= 0, row < height // 2)
        for im in range(2):
            pre = conv_row(w3_ref, x3, (im,), t) + b3_ref[...]
            cdf = phi(pre)
            put_taps(x4, (im, t), jnp.where(inside, pre * cdf, 0.0))
            if im == 0:
                s3_ref[t] = jnp.where(inside, slope_of(pre, cdf), 0.0)
        return carry

    lax.fori_loop(0, half + 2, layer_three, 0)

    def layer_four(u, carry):
        pres = [conv_row(w4_ref, x4, (im,), u) + b4_ref[...] for im in range(2)]
        cdfs = [phi(v) for v in pres]
        part, grad = lpips(
            pres[0] * cdfs[0], pres[1] * cdfs[1], l2_ref[...], float(height // 2 * (width // 2))
        )
        part2[...] += part
        g4_ref[u] = (grad * slope_of(pres[0], cdfs[0])).astype(BF16)
        return carry

    lax.fori_loop(0, half, layer_four, 0)
    loss_ref[...] = jnp.sum(part2[...], 1, keepdims=True)


def block_one_kernel(
    pre1_ref, cdf1_ref, pre2_ref, cdf2_ref, act2_ref, l1_ref, loss2_ref,
    s1_ref, gf_ref, s2_ref, loss_ref, part1, *, count,
):
    rows = pre2_ref.shape[0]

    def slopes(q, carry):
        s1_ref[q] = slope_of(pre1_ref[q + HALO - 3], cdf1_ref[q + HALO - 3])
        return carry

    lax.fori_loop(0, rows + 4, slopes, 0)
    part1[...] = jnp.zeros_like(part1)

    def row(r, carry):
        pre, cdf = pre2_ref[r], cdf2_ref[r]
        part, grad = lpips(pre * cdf, act2_ref[r], l1_ref[...], count)
        part1[...] += part
        gf_ref[r] = grad
        s2_ref[r] = slope_of(pre, cdf)
        return carry

    lax.fori_loop(0, rows, row, 0)
    loss_ref[...] = jnp.sum(part1[...], 1, keepdims=True) + loss2_ref[...]


def deep_back_kernel(
    prev_ref, own_ref, next_ref, s3_ref, gf_ref, s2_ref, w4_ref, w3_ref, up_ref, g2_ref, x5, x6
):
    half = own_ref.shape[0]
    for e in range(half + 4):
        if e < 2:
            v = prev_ref[e]
        elif e < half + 2:
            v = own_ref[e - 2]
        else:
            v = next_ref[e - half - 2]
        put_taps(x5, (e,), v.astype(F32))

    def third(t, carry):
        put_taps(x6, (t,), conv_row(w4_ref, x5, (), t) * s3_ref[t])
        return carry

    lax.fori_loop(0, half + 2, third, 0)

    def second(p, carry):
        wide = exact_dot(conv_row(w3_ref, x6, (), p), up_ref[...])
        for k in range(2):
            g2_ref[2 * p + k] = ((gf_ref[2 * p + k] + wide) * s2_ref[2 * p + k]).astype(BF16)
        return carry

    lax.fori_loop(0, half, second, 0)


def inner_back_kernel(own_ref, s1_ref, w2_ref, w1_ref, y_ref, x7):
    rows = own_ref.shape[0]
    for e in range(rows):
        put_taps(x7, (e,), own_ref[e].astype(F32))

    def first(k, carry):
        g1 = (conv_row(w2_ref, x7, (), k) * s1_ref[k + 3]).astype(BF16)
        y_ref[k] = fold_taps(dot(w1_ref[...], g1))
        return carry

    lax.fori_loop(0, rows - 2, first, 0)


def shallow_back_kernel(
    start_ref, prev_ref, own_ref, next_ref, s1_ref, w2_ref, w1_ref, f_ref, loss_ref, inner_ref,
    taps_ref, sums_ref, x7, y, *, height,
):
    rows = own_ref.shape[0]
    start = start_ref[0]
    o, shift, scale = channel_consts()
    for e in range(5):
        put_taps(x7, (0, e), (prev_ref[e] if e < 3 else own_ref[e - 3]).astype(F32))
        put_taps(x7, (1, e), (own_ref[rows - 2 + e] if e < 2 else next_ref[e - 2]).astype(F32))
    for k in range(rows - 2):
        y[k + 3] = inner_ref[k]
    for side in range(2):
        for k in range(3):
            q = k + side * (rows + 1)
            row = start + q - 2
            inside = jnp.logical_and(row >= 0, row < height)
            g1 = conv_row(w2_ref, x7, (side,), k) * s1_ref[q]
            g1 = jnp.where(inside, g1, 0.0).astype(BF16)
            y[q] = fold_taps(dot(w1_ref[...], g1))
    bias = jnp.zeros((PAD, 1), F32)
    for p in range(rows + 2):
        row = start + p - 1
        inside = jnp.logical_and(row >= 0, row < height)
        g = y[p, 0:PAD] + y[p + 1, PAD : 2 * PAD] + y[p + 2, 2 * PAD : 3 * PAD]
        g = jnp.where(inside, (g / scale).astype(BF16).astype(F32), 0.0)
        if 1 <= p <= rows:
            bias = bias + jnp.sum(g, 1, keepdims=True)
        put_taps(taps_ref, (p,), g)
    cf = f_ref.shape[1]
    totals = []
    for a in range(3):
        total = jnp.zeros((3 * PAD, cf), F32)
        for s in range(rows):
            total = total + lax.dot_general(
                taps_ref[s + 2 - a], f_ref[s], (((1,), (1,)), ((), ())), preferred_element_type=F32
            )
        totals.append(total)
    last = jnp.where(o == 7, loss_ref[...], pltpu.roll(jnp.broadcast_to(bias, (PAD, cf)), TGT, 0))
    sums_ref[0] = totals[0] + pltpu.roll(totals[1], TGT, 0)
    sums_ref[1] = totals[2]
    sums_ref[1, 0:PAD] = totals[2][0:PAD] + last


def feature_kernel(taps_ref, w_ref, out_ref):
    for r in range(out_ref.shape[0]):
        out_ref[r] = conv_row(w_ref, taps_ref, (), r).astype(BF16)


def call(kernel, n_in, outs, scratch=(), smem=()):
    return pl.pallas_call(
        kernel,
        in_specs=[
            pl.BlockSpec(memory_space=pltpu.SMEM if i in smem else pltpu.VMEM) for i in range(n_in)
        ],
        out_specs=[pl.BlockSpec(memory_space=pltpu.VMEM) for _ in outs],
        out_shape=[jax.ShapeDtypeStruct(s, t) for s, t in outs],
        scratch_shapes=[pltpu.VMEM(s, t) for s, t in scratch],
        compiler_params=pltpu.CompilerParams(vmem_limit_bytes=48 * 1024 * 1024),
    )


def flipped(weight):
    return jnp.flip(weight, (2, 3)).transpose(1, 0, 2, 3)


def taps_in(w, pad=0):
    o, i = w.shape[:2]
    w = jnp.pad(w, ((0, 0), (0, pad), (0, 0), (0, 0)))
    return w.transpose(2, 0, 3, 1).reshape(3, o, 3 * (i + pad))


def taps_out(w):
    o, i = w.shape[:2]
    w = jnp.pad(w, ((0, PAD - o), (0, 0), (0, 0), (0, 0)))
    return w.transpose(3, 2, 0, 1).reshape(9 * PAD, i)


def summed(array, axis):
    size = lax.axis_size(axis)
    if size & (size - 1):
        return lax.psum(array, axis)
    step = 1
    while step < size:
        array = array + lax.ppermute(array, axis, [(i, i ^ step) for i in range(size)])
        step *= 2
    return array


def from_neighbours(last, first):
    size = lax.axis_size("row")
    up = [(i, i + 1) for i in range(size - 1)]
    down = [(i + 1, i) for i in range(size - 1)]
    return lax.ppermute(last, "row", up), lax.ppermute(first, "row", down)


def local(
    features, out_weight, out_bias, targets, weight_one, bias_one, weight_two, bias_two,
    weight_three, bias_three, weight_four, bias_four, lin_one, lin_two,
):
    frames, cf, rows, width = features.shape
    c1 = weight_one.shape[0]
    c2 = weight_three.shape[0]
    assert frames == 1 and rows % 2 == 0 and rows > HALO
    height = rows * lax.axis_size("row")
    half, wh = rows // 2, width // 2
    edge = HALO - 4
    start = (lax.axis_index("row") * rows).astype(jnp.int32).reshape(1)

    colors = targets.shape[1]
    tgt = targets[0].astype(F32).transpose(1, 0, 2)
    tgt = jnp.pad(tgt, ((0, 0), (TGT, PAD - TGT - colors), (0, 0)))
    feat = features[0].transpose(1, 0, 2)
    band = (HALO + 1, PAD, width)
    own, top, bottom = call(
        out_conv_kernel, 3, [((rows + 2, PAD, width), F32), (band, F32), (band, F32)]
    )(feat, taps_out(out_weight), tgt)
    prev, nxt = from_neighbours(bottom, top)

    j = jnp.arange(width)[:, None] // 2 == jnp.arange(wh)[None, :]
    pool = jnp.where(j, 0.25, 0.0).astype(BF16)
    col = lambda b: b[:, None]
    ob = jnp.pad(out_bias, (0, PAD - out_bias.shape[0]))

    w1 = jnp.pad(weight_one, ((0, 0), (0, PAD - colors), (0, 0), (0, 0)))
    w1 = taps_in(jnp.concatenate([w1, jnp.roll(w1, TGT, 1)], 0))
    r1 = rows + 2 * HALO
    pre1, cdf1, pre2, cdf2, act2, s3, g4, loss = call(
        lambda *r: forward_kernel(*r, height=height), 15,
        [
            ((r1 - 2, c1, width), F32), ((r1 - 2, c1, width), F32),
            ((rows, c1, width), F32), ((rows, c1, width), F32), ((rows, c1, width), F32),
            ((half + 2, c2, wh), F32), ((half, c2, wh), BF16), ((1, 1), F32),
        ],
        [
            ((r1, 3 * PAD, width), BF16), ((2, r1 - 2, 3 * c1, width), BF16),
            ((2, half + 2 * edge, 3 * c1, wh), BF16), ((2, half + 2, 3 * c2, wh), BF16),
            ((1, wh), F32),
        ],
        smem=(0,),
    )(
        start, prev, own, nxt, col(ob),
        w1, col(bias_one), taps_in(weight_two), col(bias_two),
        taps_in(weight_three), col(bias_three), taps_in(weight_four), col(bias_four),
        col(lin_two), pool,
    )

    gprev, gnext = from_neighbours(g4[half - 2 :], g4[:2])
    s1, gf, s2, loss = call(
        lambda *r: block_one_kernel(*r, count=float(height * width)), 7,
        [
            ((rows + 4, c1, width), F32), ((rows, c1, width), F32), ((rows, c1, width), F32),
            ((1, 1), F32),
        ],
        [((1, width), F32)],
    )(pre1, cdf1, pre2, cdf2, act2, col(lin_one), loss)
    (g2,) = call(
        deep_back_kernel, 9, [((rows, c1, width), BF16)],
        [((half + 4, 3 * c2, wh), BF16), ((half + 2, 3 * c2, wh), BF16)],
    )(gprev, g4, gnext, s3, gf, s2, taps_in(flipped(weight_four)), taps_in(flipped(weight_three)), pool.T)

    g2prev, g2next = from_neighbours(g2[rows - 3 :], g2[:3])
    w2_back, w1_back = taps_in(flipped(weight_two)), taps_out(flipped(weight_one))
    (inner,) = call(
        inner_back_kernel, 4, [((rows - 2, 3 * PAD, width), F32)], [((rows, 3 * c1, width), BF16)]
    )(g2, s1, w2_back, w1_back)
    taps, sums = call(
        lambda *r: shallow_back_kernel(*r, height=height), 10,
        [((rows + 2, 3 * PAD, width), BF16), ((2, 3 * PAD, cf), F32)],
        [((2, 5, 3 * c1, width), BF16), ((rows + 4, 3 * PAD, width), F32)],
        smem=(0,),
    )(start, g2prev, g2, g2next, s1, w2_back, w1_back, feat, loss, inner)
    sums = summed(summed(sums, "row"), "clip")
    (fg,) = call(feature_kernel, 2, [((rows, cf, width), BF16)])(
        taps, taps_in(flipped(out_weight), PAD - out_weight.shape[0])
    )
    feature_grad = fg.transpose(1, 0, 2)[None]
    loss = sums[1, TGT + 3, 0]
    bias_grad = sums[1, TGT : TGT + colors, 0]
    sums = sums.reshape(2, 3, PAD, cf)[:, ::-1]
    wg = jnp.stack([sums[0, :, :colors], sums[0, :, TGT : TGT + colors], sums[1, :, :colors]])
    return (loss, feature_grad, wg.transpose(2, 3, 0, 1), bias_grad)


def solution(mesh):
    tile = P("clip", None, "row", None)
    return jax.shard_map(
        local,
        mesh=mesh,
        in_specs=(tile, P(), P(), tile) + (P(),) * 10,
        out_specs=(P(), tile, P(), P()),
        check_vma=False,
    )
```

```python
import math

import jax
import jax.numpy as jnp
from jax import lax
from jax.experimental import pallas as pl
from jax.experimental.pallas import tpu as pltpu
from jax.sharding import PartitionSpec as P

shift_values = [-0.03, -0.088, -0.188]
scale_values = [0.458, 0.448, 0.45]
PAD = 8
TGT = 4
HALO = 6
F32 = jnp.float32
BF16 = jnp.bfloat16

erf_top = [0.00022905065861350646, 0.0034082910107109506, 0.050955695062380861, 0.18520832239976145, 1.128379143519084]
erf_bottom = [-1.1791602954361697e-7, 0.000023547966471313185, 0.0010179625278914885, 0.014070470171167667, 0.11098505178285362, 0.49746925110067538, 1.0]


def poly(x, coefs):
    total = jnp.full_like(x, coefs[0])
    for c in coefs[1:]:
        total = total * x + c
    return total


LIMIT = 3.832506856900711 * math.sqrt(2.0)
phi_top = [c * 0.5**k * 0.5 * math.sqrt(0.5) for k, c in zip(range(4, -1, -1), erf_top)]
phi_bottom = [c * 0.5**k for k, c in zip(range(6, -1, -1), erf_bottom)]


def phi(v):
    x = jnp.clip(v, -LIMIT, LIMIT)
    sq = x * x
    return 0.5 + x * poly(sq, phi_top) / poly(sq, phi_bottom)


def slope_of(v, cdf):
    return cdf + v * (jnp.exp(-0.5 * v * v) * (1.0 / math.sqrt(2.0 * math.pi)))


def dot(a, b):
    return jnp.dot(a, b, preferred_element_type=F32)


def left_right(x):
    width = x.shape[1]
    col = lax.broadcasted_iota(jnp.int32, x.shape, 1)
    left = jnp.where(col == 0, 0.0, pltpu.roll(x, 1, 1))
    right = jnp.where(col == width - 1, 0.0, pltpu.roll(x, width - 1, 1))
    return left, right


def put_taps(ref, where, x):
    c = x.shape[0]
    left, right = left_right(x)
    if c % 16:
        ref[where] = jnp.concatenate([left, x, right], 0).astype(BF16)
    else:
        ref[where + (slice(0, c),)] = left.astype(BF16)
        ref[where + (slice(c, 2 * c),)] = x.astype(BF16)
        ref[where + (slice(2 * c, 3 * c),)] = right.astype(BF16)


def fold_taps(y):
    n = y.shape[0] // 3
    width = y.shape[1]
    col = lax.broadcasted_iota(jnp.int32, (n, width), 1)
    left = jnp.where(col == 0, 0.0, pltpu.roll(y[:n], 1, 1))
    right = jnp.where(col == width - 1, 0.0, pltpu.roll(y[2 * n :], width - 1, 1))
    return left + y[n : 2 * n] + right


def conv_row(w_ref, x_ref, where, row):
    total = dot(w_ref[0], x_ref[where + (row,)])
    for a in (1, 2):
        total = total + dot(w_ref[a], x_ref[where + (row + a,)])
    return total


def two_parts(x):
    high = x.astype(BF16)
    low = (x - high.astype(F32)).astype(BF16)
    return high, low


def exact_dot(x, m):
    high, low = two_parts(x)
    return dot(high, m) + dot(low, m)


def lpips(dec, tgt, lin, count):
    inv_dec = 1.0 / jnp.sqrt(jnp.sum(dec * dec, 0, keepdims=True) + 1e-06)
    inv_tgt = 1.0 / jnp.sqrt(jnp.sum(tgt * tgt, 0, keepdims=True) + 1e-06)
    unit = dec * inv_dec
    differ = unit - tgt * inv_tgt
    weighted = lin * differ
    part = jnp.sum(weighted * differ, 0, keepdims=True) * (1.0 / count)
    grad = weighted * (2.0 / count)
    along = jnp.sum(grad * unit, 0, keepdims=True)
    return part, (grad - unit * along) * inv_dec


def channel_consts():
    o = lax.broadcasted_iota(jnp.int32, (PAD, 1), 0)

    def pick(values, other):
        out = jnp.full((PAD, 1), other, F32)
        for i, v in enumerate(values):
            out = jnp.where(o % TGT == i, v, out)
        return out

    return o, pick(shift_values, 0.0), pick(scale_values, 1.0)


def out_conv_kernel(f_ref, w_ref, t_ref, own_ref, top_ref, bottom_ref):
    rows = f_ref.shape[0]
    width = f_ref.shape[2]
    folded = [fold_taps(dot(w_ref[...], f_ref[s])) for s in range(rows)]
    out = []
    for t in range(rows + 2):
        total = jnp.zeros((PAD, width), F32)
        for a in range(3):
            s = t + a - 2
            if 0 <= s < rows:
                total = total + folded[s][a * PAD : (a + 1) * PAD]
        if 1 <= t <= rows:
            total = total + t_ref[t - 1]
        out.append(total)
        own_ref[t] = total
    for k in range(HALO + 1):
        top_ref[k] = out[k]
        bottom_ref[k] = out[rows + 2 - (HALO + 1) + k]


def forward_kernel(
    start_ref, prev_ref, own_ref, next_ref, ob_ref,
    w1_ref, b1_ref, w2_ref, b2_ref, w3_ref, b3_ref, w4_ref, b4_ref, l2_ref, pool_ref,
    pre1_ref, cdf1_ref, pre2_ref, cdf2_ref, act2_ref, s3_ref, g4_ref, loss_ref,
    x1, x2, x3, x4, part2, *, height,
):
    rows = own_ref.shape[0] - 2
    width = own_ref.shape[2]
    start = start_ref[0]
    o, shift, scale = channel_consts()

    def image(v, row):
        im = ((v.astype(BF16).astype(F32) - shift) / scale).astype(BF16).astype(F32)
        inside = jnp.logical_and(row >= 0, row < height)
        return jnp.where(jnp.logical_and(o % TGT < 3, inside), im, 0.0)

    for e in range(rows + 2 * HALO):
        v = jnp.zeros((PAD, width), F32)
        if HALO - 1 <= e < HALO + rows + 1:
            v = v + own_ref[e - HALO + 1]
        if e < HALO + 1:
            v = v + prev_ref[e]
        if e >= HALO + rows - 1:
            v = v + next_ref[e - (HALO + rows - 1)]
        put_taps(x1, (e,), image(v + ob_ref[...], start + e - HALO))

    def layer_one(q, carry):
        row = start + q - (HALO - 1)
        inside = jnp.logical_and(row >= 0, row < height)
        both = conv_row(w1_ref, x1, (), q)
        c1 = b1_ref.shape[0]
        for im in range(2):
            pre = both[im * c1 : (im + 1) * c1] + b1_ref[...]
            cdf = phi(pre)
            put_taps(x2, (im, q), jnp.where(inside, pre * cdf, 0.0))
            if im == 0:
                pre1_ref[q] = pre
                cdf1_ref[q] = cdf
        return carry

    lax.fori_loop(0, rows + 2 * HALO - 2, layer_one, 0, unroll=2)

    part2[...] = jnp.zeros_like(part2)
    half = rows // 2
    edge = HALO - 4

    def layer_two(p, carry):
        row = start // 2 + p - edge
        inside = jnp.logical_and(row >= 0, row < height // 2)
        pres = [[conv_row(w2_ref, x2, (im,), 2 * p + k) + b2_ref[...] for k in range(2)] for im in range(2)]
        cdfs = [[phi(pres[im][k]) for k in range(2)] for im in range(2)]
        acts = [[pres[im][k] * cdfs[im][k] for k in range(2)] for im in range(2)]
        for im in range(2):
            pooled = exact_dot(acts[im][0] + acts[im][1], pool_ref[...])
            put_taps(x3, (im, p), jnp.where(inside, pooled, 0.0))

        @pl.when(jnp.logical_and(p >= edge, p < edge + half))
        def _():
            for k in range(2):
                pre2_ref[2 * (p - edge) + k] = pres[0][k]
                cdf2_ref[2 * (p - edge) + k] = cdfs[0][k]
                act2_ref[2 * (p - edge) + k] = acts[1][k]

        return carry

    lax.fori_loop(0, half + 2 * edge, layer_two, 0, unroll=2)

    def layer_three(t, carry):
        row = start // 2 + t - (edge - 1)
        inside = jnp.logical_and(row >= 0, row < height // 2)
        for im in range(2):
            pre = conv_row(w3_ref, x3, (im,), t) + b3_ref[...]
            cdf = phi(pre)
            put_taps(x4, (im, t), jnp.where(inside, pre * cdf, 0.0))
            if im == 0:
                s3_ref[t] = jnp.where(inside, slope_of(pre, cdf), 0.0)
        return carry

    lax.fori_loop(0, half + 2, layer_three, 0, unroll=2)

    def layer_four(u, carry):
        pres = [conv_row(w4_ref, x4, (im,), u) + b4_ref[...] for im in range(2)]
        cdfs = [phi(v) for v in pres]
        part, grad = lpips(
            pres[0] * cdfs[0], pres[1] * cdfs[1], l2_ref[...], float(height // 2 * (width // 2))
        )
        part2[...] += part
        g4_ref[u] = (grad * slope_of(pres[0], cdfs[0])).astype(BF16)
        return carry

    lax.fori_loop(0, half, layer_four, 0, unroll=2)
    loss_ref[...] = jnp.sum(part2[...], 1, keepdims=True)


def block_one_kernel(
    pre1_ref, cdf1_ref, pre2_ref, cdf2_ref, act2_ref, l1_ref, loss2_ref,
    s1_ref, gf_ref, s2_ref, loss_ref, part1, *, count,
):
    rows = pre2_ref.shape[0]

    def slopes(q, carry):
        s1_ref[q] = slope_of(pre1_ref[q + HALO - 3], cdf1_ref[q + HALO - 3])
        return carry

    lax.fori_loop(0, rows + 4, slopes, 0, unroll=2)
    part1[...] = jnp.zeros_like(part1)

    def row(r, carry):
        pre, cdf = pre2_ref[r], cdf2_ref[r]
        part, grad = lpips(pre * cdf, act2_ref[r], l1_ref[...], count)
        part1[...] += part
        gf_ref[r] = grad
        s2_ref[r] = slope_of(pre, cdf)
        return carry

    lax.fori_loop(0, rows, row, 0, unroll=2)
    loss_ref[...] = jnp.sum(part1[...], 1, keepdims=True) + loss2_ref[...]


def deep_back_kernel(
    prev_ref, own_ref, next_ref, s3_ref, gf_ref, s2_ref, w4_ref, w3_ref, up_ref, g2_ref, x5, x6
):
    half = own_ref.shape[0]
    for e in range(half + 4):
        if e < 2:
            v = prev_ref[e]
        elif e < half + 2:
            v = own_ref[e - 2]
        else:
            v = next_ref[e - half - 2]
        put_taps(x5, (e,), v.astype(F32))

    def third(t, carry):
        put_taps(x6, (t,), conv_row(w4_ref, x5, (), t) * s3_ref[t])
        return carry

    lax.fori_loop(0, half + 2, third, 0, unroll=2)

    def second(p, carry):
        wide = exact_dot(conv_row(w3_ref, x6, (), p), up_ref[...])
        for k in range(2):
            g2_ref[2 * p + k] = ((gf_ref[2 * p + k] + wide) * s2_ref[2 * p + k]).astype(BF16)
        return carry

    lax.fori_loop(0, half, second, 0, unroll=2)


def inner_back_kernel(own_ref, s1_ref, w2_ref, w1_ref, y_ref, x7):
    rows = own_ref.shape[0]
    for e in range(rows):
        put_taps(x7, (e,), own_ref[e].astype(F32))

    def first(k, carry):
        g1 = (conv_row(w2_ref, x7, (), k) * s1_ref[k + 3]).astype(BF16)
        y_ref[k] = fold_taps(dot(w1_ref[...], g1))
        return carry

    lax.fori_loop(0, rows - 2, first, 0, unroll=2)


def shallow_back_kernel(
    start_ref, prev_ref, own_ref, next_ref, s1_ref, w2_ref, w1_ref, f_ref, loss_ref, inner_ref,
    taps_ref, sums_ref, x7, y, *, height,
):
    rows = own_ref.shape[0]
    start = start_ref[0]
    o, shift, scale = channel_consts()
    for e in range(5):
        put_taps(x7, (0, e), (prev_ref[e] if e < 3 else own_ref[e - 3]).astype(F32))
        put_taps(x7, (1, e), (own_ref[rows - 2 + e] if e < 2 else next_ref[e - 2]).astype(F32))
    for k in range(rows - 2):
        y[k + 3] = inner_ref[k]
    for side in range(2):
        for k in range(3):
            q = k + side * (rows + 1)
            row = start + q - 2
            inside = jnp.logical_and(row >= 0, row < height)
            g1 = conv_row(w2_ref, x7, (side,), k) * s1_ref[q]
            g1 = jnp.where(inside, g1, 0.0).astype(BF16)
            y[q] = fold_taps(dot(w1_ref[...], g1))
    bias = jnp.zeros((PAD, 1), F32)
    for p in range(rows + 2):
        row = start + p - 1
        inside = jnp.logical_and(row >= 0, row < height)
        g = y[p, 0:PAD] + y[p + 1, PAD : 2 * PAD] + y[p + 2, 2 * PAD : 3 * PAD]
        g = jnp.where(inside, (g / scale).astype(BF16).astype(F32), 0.0)
        if 1 <= p <= rows:
            bias = bias + jnp.sum(g, 1, keepdims=True)
        put_taps(taps_ref, (p,), g)
    cf = f_ref.shape[1]
    totals = []
    for a in range(3):
        total = jnp.zeros((3 * PAD, cf), F32)
        for s in range(rows):
            total = total + lax.dot_general(
                taps_ref[s + 2 - a], f_ref[s], (((1,), (1,)), ((), ())), preferred_element_type=F32
            )
        totals.append(total)
    last = jnp.where(o == 7, loss_ref[...], pltpu.roll(jnp.broadcast_to(bias, (PAD, cf)), TGT, 0))
    sums_ref[0] = totals[0] + pltpu.roll(totals[1], TGT, 0)
    sums_ref[1] = totals[2]
    sums_ref[1, 0:PAD] = totals[2][0:PAD] + last


def feature_kernel(taps_ref, w_ref, out_ref):
    for r in range(out_ref.shape[0]):
        out_ref[r] = conv_row(w_ref, taps_ref, (), r).astype(BF16)


def call(kernel, n_in, outs, scratch=(), smem=()):
    return pl.pallas_call(
        kernel,
        in_specs=[
            pl.BlockSpec(memory_space=pltpu.SMEM if i in smem else pltpu.VMEM) for i in range(n_in)
        ],
        out_specs=[pl.BlockSpec(memory_space=pltpu.VMEM) for _ in outs],
        out_shape=[jax.ShapeDtypeStruct(s, t) for s, t in outs],
        scratch_shapes=[pltpu.VMEM(s, t) for s, t in scratch],
        compiler_params=pltpu.CompilerParams(vmem_limit_bytes=48 * 1024 * 1024),
    )


def flipped(weight):
    return jnp.flip(weight, (2, 3)).transpose(1, 0, 2, 3)


def taps_in(w, pad=0):
    o, i = w.shape[:2]
    w = jnp.pad(w, ((0, 0), (0, pad), (0, 0), (0, 0)))
    return w.transpose(2, 0, 3, 1).reshape(3, o, 3 * (i + pad))


def taps_out(w):
    o, i = w.shape[:2]
    w = jnp.pad(w, ((0, PAD - o), (0, 0), (0, 0), (0, 0)))
    return w.transpose(3, 2, 0, 1).reshape(9 * PAD, i)


def summed(array, axis):
    size = lax.axis_size(axis)
    if size & (size - 1):
        return lax.psum(array, axis)
    step = 1
    while step < size:
        array = array + lax.ppermute(array, axis, [(i, i ^ step) for i in range(size)])
        step *= 2
    return array


def from_neighbours(last, first):
    size = lax.axis_size("row")
    up = [(i, i + 1) for i in range(size - 1)]
    down = [(i + 1, i) for i in range(size - 1)]
    return lax.ppermute(last, "row", up), lax.ppermute(first, "row", down)


def local(
    features, out_weight, out_bias, targets, weight_one, bias_one, weight_two, bias_two,
    weight_three, bias_three, weight_four, bias_four, lin_one, lin_two,
):
    frames, cf, rows, width = features.shape
    c1 = weight_one.shape[0]
    c2 = weight_three.shape[0]
    assert frames == 1 and rows % 2 == 0 and rows > HALO
    height = rows * lax.axis_size("row")
    half, wh = rows // 2, width // 2
    edge = HALO - 4
    start = (lax.axis_index("row") * rows).astype(jnp.int32).reshape(1)

    colors = targets.shape[1]
    tgt = targets[0].astype(F32).transpose(1, 0, 2)
    tgt = jnp.pad(tgt, ((0, 0), (TGT, PAD - TGT - colors), (0, 0)))
    feat = features[0].transpose(1, 0, 2)
    band = (HALO + 1, PAD, width)
    own, top, bottom = call(
        out_conv_kernel, 3, [((rows + 2, PAD, width), F32), (band, F32), (band, F32)]
    )(feat, taps_out(out_weight), tgt)
    prev, nxt = from_neighbours(bottom, top)

    j = jnp.arange(width)[:, None] // 2 == jnp.arange(wh)[None, :]
    pool = jnp.where(j, 0.25, 0.0).astype(BF16)
    col = lambda b: b[:, None]
    ob = jnp.pad(out_bias, (0, PAD - out_bias.shape[0]))

    w1 = jnp.pad(weight_one, ((0, 0), (0, PAD - colors), (0, 0), (0, 0)))
    w1 = taps_in(jnp.concatenate([w1, jnp.roll(w1, TGT, 1)], 0))
    r1 = rows + 2 * HALO
    pre1, cdf1, pre2, cdf2, act2, s3, g4, loss = call(
        lambda *r: forward_kernel(*r, height=height), 15,
        [
            ((r1 - 2, c1, width), F32), ((r1 - 2, c1, width), F32),
            ((rows, c1, width), F32), ((rows, c1, width), F32), ((rows, c1, width), F32),
            ((half + 2, c2, wh), F32), ((half, c2, wh), BF16), ((1, 1), F32),
        ],
        [
            ((r1, 3 * PAD, width), BF16), ((2, r1 - 2, 3 * c1, width), BF16),
            ((2, half + 2 * edge, 3 * c1, wh), BF16), ((2, half + 2, 3 * c2, wh), BF16),
            ((1, wh), F32),
        ],
        smem=(0,),
    )(
        start, prev, own, nxt, col(ob),
        w1, col(bias_one), taps_in(weight_two), col(bias_two),
        taps_in(weight_three), col(bias_three), taps_in(weight_four), col(bias_four),
        col(lin_two), pool,
    )

    gprev, gnext = from_neighbours(g4[half - 2 :], g4[:2])
    s1, gf, s2, loss = call(
        lambda *r: block_one_kernel(*r, count=float(height * width)), 7,
        [
            ((rows + 4, c1, width), F32), ((rows, c1, width), F32), ((rows, c1, width), F32),
            ((1, 1), F32),
        ],
        [((1, width), F32)],
    )(pre1, cdf1, pre2, cdf2, act2, col(lin_one), loss)
    (g2,) = call(
        deep_back_kernel, 9, [((rows, c1, width), BF16)],
        [((half + 4, 3 * c2, wh), BF16), ((half + 2, 3 * c2, wh), BF16)],
    )(gprev, g4, gnext, s3, gf, s2, taps_in(flipped(weight_four)), taps_in(flipped(weight_three)), pool.T)

    g2prev, g2next = from_neighbours(g2[rows - 3 :], g2[:3])
    w2_back, w1_back = taps_in(flipped(weight_two)), taps_out(flipped(weight_one))
    (inner,) = call(
        inner_back_kernel, 4, [((rows - 2, 3 * PAD, width), F32)], [((rows, 3 * c1, width), BF16)]
    )(g2, s1, w2_back, w1_back)
    taps, sums = call(
        lambda *r: shallow_back_kernel(*r, height=height), 10,
        [((rows + 2, 3 * PAD, width), BF16), ((2, 3 * PAD, cf), F32)],
        [((2, 5, 3 * c1, width), BF16), ((rows + 4, 3 * PAD, width), F32)],
        smem=(0,),
    )(start, g2prev, g2, g2next, s1, w2_back, w1_back, feat, loss, inner)
    sums = summed(summed(sums, "row"), "clip")
    (fg,) = call(feature_kernel, 2, [((rows, cf, width), BF16)])(
        taps, taps_in(flipped(out_weight), PAD - out_weight.shape[0])
    )
    feature_grad = fg.transpose(1, 0, 2)[None]
    loss = sums[1, TGT + 3, 0]
    bias_grad = sums[1, TGT : TGT + colors, 0]
    sums = sums.reshape(2, 3, PAD, cf)[:, ::-1]
    wg = jnp.stack([sums[0, :, :colors], sums[0, :, TGT : TGT + colors], sums[1, :, :colors]])
    return (loss, feature_grad, wg.transpose(2, 3, 0, 1), bias_grad)


def solution(mesh):
    tile = P("clip", None, "row", None)
    return jax.shard_map(
        local,
        mesh=mesh,
        in_specs=(tile, P(), P(), tile) + (P(),) * 10,
        out_specs=(P(), tile, P(), P()),
        check_vma=False,
    )
```
